256 devices in a mesh: dp: 32 (over y, x, core), filter: 8 (over z).
Axes of the slice: x: 4, y: 4, z: 8, core: 2. Of those that a mesh axis runs over, the one named last changes fastest.
Arguments:
- inputs: bfloat16 [32, 48, 24, 1024], P('dp', None, None, 'filter'), may hold values from -6 to 6
- kernel: bfloat16 [3, 3, 1024, 1024], P(None, None, 'filter'), may hold values from -0.0625 to 0.0625
- cotangent: bfloat16 [32, 48, 24, 1024], P('dp', 'filter'), may hold values from -6 to 6
Outputs:
- outputs: bfloat16 [32, 48, 24, 1024], P('dp', 'filter')
- input_grad: bfloat16 [32, 48, 24, 1024], P('dp', None, None, 'filter')
- kernel_grad: float32 [1024, 3, 3, 1024], P('dp', None, None, 'filter')
The draws below stay inside these ranges and needn't reach their ends.
All inputs are finite; a program needn't handle non-finite values.
Results may differ from the reference program's by a relative error of at most 0.001.
Values may be sent and summed in bfloat16 or wider, within the bound.
No kernel may reach another device: no remote copies, remote signals or barrier semaphores. Data moves between devices by JAX's collectives and lax.ppermute only.
A program may use at most 128 MiB of HBM per device.

```python
import jax
import jax.numpy as jnp
from jax import lax

C = 1024
H = 48
W = 24
BATCH = 32


def strengthened(drawn, key, source, target, parts, factor):
    owner, partner = [(jnp.arange(drawn.shape[dim]) // (drawn.shape[dim] // parts)).reshape([-1 if axis == dim else 1 for axis in range(drawn.ndim)]) for dim in (source, target)]
    chosen = jax.random.permutation(key, parts)[partner]
    strong = (owner == chosen) | (owner == (partner + parts // 2) % parts)
    return jnp.where(strong, factor * drawn, drawn)


def level_of(rng, shape, split, least, top_value):
    gain, own = 1.0, jax.random.fold_in(rng, 6)
    for position, blocks in split:
        steps = jnp.exp(jax.random.uniform(jax.random.fold_in(own, position), (blocks,), jnp.float32, least / len(split), top_value / len(split)))
        gain = gain * jnp.repeat(steps, shape[position] // blocks).reshape([-1 if axis == position else 1 for axis in range(len(shape))])
    return gain


def bell_draw(rng, dims, spread, reach, cuts=(), kind=jnp.bfloat16):
    array = spread * jax.random.normal(rng, dims, jnp.float32)
    if cuts:
        array = array * level_of(rng, dims, cuts, -0.22, 0.18)
    return jnp.clip(array, -reach, reach).astype(kind)


def heavy_noise(own_key, extent, deviation, bound, pieces, heavy, held_as=jnp.bfloat16):
    values = deviation * jax.random.normal(own_key, extent, jnp.float32)
    if pieces:
        values = values * level_of(own_key, extent, pieces, -0.22, 0.18)
    return jnp.clip(strengthened(values, jax.random.fold_in(own_key, 3), *heavy), -bound, bound).astype(held_as)


def setup_inputs(seed: int = 0) -> dict:
    streams_of = jax.random.split(jax.random.key(seed), 4)
    return {
        "inputs": heavy_noise(streams_of[0], (BATCH, H, W, C), 1.0, 6.0, ((0, 32), (3, 8)), (3, 1, 8, 2.0)),
        "kernel": bell_draw(streams_of[1], (3, 3, C, C), (9 * C) ** -0.5, 0.0625, ((2, 8),)),
        "cotangent": heavy_noise(streams_of[2], (BATCH, H, W, C), 1.0, 6.0, ((0, 32), (1, 8)), (0, 3, 32, 2.75)),
    }


def one_sample(carry, pair):
    sample, grad_out = pair
    kernel_f = carry[1]
    xpad = jnp.pad(sample.astype(jnp.float32), ((1, 1), (1, 1), (0, 0)))
    gpad = jnp.pad(grad_out.astype(jnp.float32), ((1, 1), (1, 1), (0, 0)))
    result = jnp.zeros((H, W, C), jnp.float32)
    back = jnp.zeros((H, W, C), jnp.float32)
    taps = []
    for a in range(3):
        for b in range(3):
            result = result + jnp.einsum('hwi,io->hwo', xpad[a:a + H, b:b + W], kernel_f[a, b])
            back = back + jnp.einsum('hwo,io->hwi', gpad[2 - a:2 - a + H, 2 - b:2 - b + W], kernel_f[a, b])
            taps.append(jnp.einsum('hwi,hwo->oi', xpad[a:a + H, b:b + W], grad_out.astype(jnp.float32)))
    grads = jnp.stack(taps, 1).reshape(C, 3, 3, C)
    return ((carry[0] + grads, kernel_f), (result.astype(jnp.bfloat16), back.astype(jnp.bfloat16)))

def reference(inputs, kernel, cotangent):
    kernel_f = kernel.astype(jnp.float32)
    start = (jnp.zeros((C, 3, 3, C), jnp.float32), kernel_f)
    final, (outputs, input_grad) = lax.scan(one_sample, start, (inputs, cotangent))
    scale = 1.0 / jnp.sqrt(jnp.float32(BATCH * H * W))
    return (outputs, input_grad, final[0] * scale)
```

```python
import functools

import jax
import jax.numpy as jnp
from jax import lax
from jax.experimental import pallas as pl
from jax.experimental.pallas import tpu as pltpu
from jax.sharding import Mesh, PartitionSpec as P

F32 = jnp.float32
BF16 = jnp.bfloat16
F16 = jnp.float16
STEPS = (64, 32, 16, 8, 4, 2, 1)


def build_patches(width, x_ref, pad_ref, patch_ref):
    cells, chans = x_ref.shape
    value = x_ref[...].astype(F32)
    column = lax.rem(lax.broadcasted_iota(jnp.int32, value.shape, 0), width)
    left = jnp.where(column == 0, 0.0, pltpu.roll(value, 1, 0))
    right = jnp.where(column == width - 1, 0.0, pltpu.roll(value, cells - 1, 0))
    for b, shifted in enumerate((left, value, right)):
        pad_ref[b, :width, :] = jnp.zeros((width, chans), BF16)
        pad_ref[b, width : width + cells, :] = shifted.astype(BF16)
        pad_ref[b, width + cells :, :] = jnp.zeros((width, chans), BF16)
    for a in range(3):
        for b in range(3):
            tap = 3 * a + b
            patch_ref[:, tap * chans : (tap + 1) * chans] = pad_ref[
                b, a * width : a * width + cells, :
            ]


def forward_kernel(width, x_ref, kernel_ref, out_ref, pad_ref, patch_ref):
    @pl.when(pl.program_id(0) == 0)
    def _():
        build_patches(width, x_ref, pad_ref, patch_ref)

    out_ref[...] = jnp.dot(patch_ref[...], kernel_ref[...], preferred_element_type=F32)


def forward_partial(width, x, weights):
    cells, chans = x.shape
    taps, channels = weights.shape
    block = channels // 4
    x = pltpu.with_memory_space_constraint(x, pltpu.HBM)
    weights = pltpu.with_memory_space_constraint(weights, pltpu.HBM)
    return pl.pallas_call(
        functools.partial(forward_kernel, width),
        out_shape=pltpu.HBM((cells, channels), F32),
        grid=(4,),
        in_specs=[
            pl.BlockSpec((cells, chans), lambda i: (0, 0)),
            pl.BlockSpec((taps, block), lambda i: (0, i)),
        ],
        out_specs=pl.BlockSpec((cells, block), lambda i: (0, i)),
        scratch_shapes=[
            pltpu.VMEM((3, cells + 2 * width, chans), BF16),
            pltpu.VMEM((cells, taps), BF16),
        ],
        compiler_params=pltpu.CompilerParams(vmem_limit_bytes=16 << 20),
        name="forward",
    )(x, weights)


def exponent(top):
    power = jnp.ones_like(top)
    count = jnp.zeros_like(top)
    for step in STEPS:
        fits = top * (2.0**step) < 32768.0
        factor = jnp.where(fits, 2.0**step, 1.0)
        top = top * factor
        power = power * factor
        count = count + jnp.where(fits, float(step), 0.0)
    return power, count


def inverse(count):
    power = jnp.ones_like(count)
    for step in STEPS:
        has = count >= step
        power = power * jnp.where(has, 2.0**-step, 1.0)
        count = count - jnp.where(has, float(step), 0.0)
    return power


def split_kernel(cores, share, core_ref, cot_ref, out_ref):
    rows, channels = cot_ref.shape
    half = channels // cores
    source = lax.broadcasted_iota(jnp.int32, (channels, half), 0)
    target = lax.broadcasted_iota(jnp.int32, (channels, half), 1)
    place = (target // share) * (cores * share) + lax.rem(target, share)
    core = core_ref[0]
    top = jnp.max(jnp.abs(cot_ref[...].astype(F32)), axis=0, keepdims=True)
    top = jnp.max(top, axis=1, keepdims=True)
    power, count = exponent(jnp.broadcast_to(top, (8, half)))
    for slot, owner in ((0, 1 - core), (1, core)):
        pick = jnp.where(source == place + owner * share, 1.0, 0.0).astype(BF16)
        value = jnp.dot(cot_ref[...], pick, preferred_element_type=F32)
        out_ref[slot, :rows, :] = value * power[:1]
        out_ref[slot, rows:, :] = count


def split_by_core(core, cot, share):
    rows, channels = cot.shape
    return pl.pallas_call(
        functools.partial(split_kernel, 2, share),
        out_shape=jax.ShapeDtypeStruct((2, rows + 8, channels // 2), F32),
        in_specs=[
            pl.BlockSpec(memory_space=pltpu.SMEM),
            pl.BlockSpec(memory_space=pltpu.VMEM),
        ],
        out_specs=pl.BlockSpec(memory_space=pltpu.VMEM),
        compiler_params=pltpu.CompilerParams(vmem_limit_bytes=16 << 20),
        name="split_by_core",
    )(core, cot)


def multiply_turned(scale, cot_ref, patch_ref, grad_ref, turned_ref):
    turned = cot_ref[...].T
    turned_ref[...] = turned
    grad = scale * jnp.dot(turned, patch_ref[...], preferred_element_type=F32)
    chips, taps, share, chans = grad_ref.shape
    for chip in range(chips):
        for tap in range(taps):
            grad_ref[chip, tap] = grad[
                chip * share : (chip + 1) * share, tap * chans : (tap + 1) * chans
            ]


def first_kernel(width, scale, x_ref, all_ref, *refs):
    grad_ref, turned_ref, mine_ref, patch_ref, pad_ref, cot_ref = refs
    build_patches(width, x_ref, pad_ref, patch_ref)
    groups, _, rows, _ = all_ref.shape
    rows = rows - 8
    for slot, ref in ((0, cot_ref), (1, mine_ref)):
        for group in range(groups):
            power = inverse(all_ref[group, slot, rows:, :].astype(F32))
            value = all_ref[group, slot, :rows, :].astype(F32) * power[:1]
            ref[group * rows : (group + 1) * rows, :] = value.astype(BF16)
    multiply_turned(scale, cot_ref, patch_ref, grad_ref, turned_ref)


def weight_first(width, scale, share, x, gathered):
    cells, chans = x.shape
    half = gathered.shape[3]
    vmem = pl.BlockSpec(memory_space=pltpu.VMEM)
    return pl.pallas_call(
        functools.partial(first_kernel, width, scale),
        out_shape=(
            jax.ShapeDtypeStruct((half // share, 9, share, chans), F32),
            jax.ShapeDtypeStruct((half, cells), BF16),
            jax.ShapeDtypeStruct((cells, half), BF16),
            jax.ShapeDtypeStruct((cells, 9 * chans), BF16),
        ),
        in_specs=[vmem, vmem],
        out_specs=(vmem,) * 4,
        scratch_shapes=[
            pltpu.VMEM((3, cells + 2 * width, chans), BF16),
            pltpu.VMEM((cells, half), BF16),
        ],
        compiler_params=pltpu.CompilerParams(vmem_limit_bytes=24 << 20),
        name="weight_first",
    )(x, gathered)


def second_kernel(scale, cot_ref, patch_ref, grad_ref, turned_ref):
    multiply_turned(scale, cot_ref, patch_ref, grad_ref, turned_ref)


def weight_second(scale, share, cot, patches):
    cells, half = cot.shape
    chans = patches.shape[1] // 9
    vmem = pl.BlockSpec(memory_space=pltpu.VMEM)
    return pl.pallas_call(
        functools.partial(second_kernel, scale),
        out_shape=(
            jax.ShapeDtypeStruct((half // share, 9, share, chans), F32),
            jax.ShapeDtypeStruct((half, cells), BF16),
        ),
        in_specs=[vmem, vmem],
        out_specs=(vmem, vmem),
        compiler_params=pltpu.CompilerParams(vmem_limit_bytes=24 << 20),
        name="weight_second",
    )(cot, patches)


def input_kernel(width, share, core_ref, theirs_ref, mine_ref, kernel_ref, out_ref, cot_ref):
    cells, chans = out_ref.shape
    chips = theirs_ref.shape[0] // share
    core = core_ref[0]
    for ref, owner in ((theirs_ref, 1 - core), (mine_ref, core)):
        for chip in range(chips):
            start = pl.multiple_of((2 * chip + owner) * share, share)
            cot_ref[pl.ds(start, share), :] = ref[chip * share : (chip + 1) * share, :]
    spread = jnp.dot(kernel_ref[...], cot_ref[...], preferred_element_type=F32)
    cell = lax.broadcasted_iota(jnp.int32, (chans, cells), 1)
    column = lax.rem(cell, width)
    total = None
    for b in range(3):
        part = None
        for a in range(3):
            tap = 3 * a + b
            term = spread[tap * chans : (tap + 1) * chans, :]
            if a == 0:
                term = jnp.where(cell < cells - width, pltpu.roll(term, cells - width, 1), 0.0)
            if a == 2:
                term = jnp.where(cell >= width, pltpu.roll(term, width, 1), 0.0)
            part = term if part is None else part + term
        if b == 0:
            part = jnp.where(column < width - 1, pltpu.roll(part, cells - 1, 1), 0.0)
        if b == 2:
            part = jnp.where(column > 0, pltpu.roll(part, 1, 1), 0.0)
        total = part if total is None else total + part
    out_ref[...] = total.T.astype(BF16)


def input_gradient(width, share, core, theirs, mine, weights):
    cells = theirs.shape[1]
    chans = weights.shape[0] // 9
    vmem = pl.BlockSpec(memory_space=pltpu.VMEM)
    return pl.pallas_call(
        functools.partial(input_kernel, width, share),
        out_shape=jax.ShapeDtypeStruct((cells, chans), BF16),
        in_specs=[pl.BlockSpec(memory_space=pltpu.SMEM)] + [vmem] * 3,
        out_specs=vmem,
        scratch_shapes=[pltpu.VMEM((weights.shape[1], cells), BF16)],
        compiler_params=pltpu.CompilerParams(vmem_limit_bytes=24 << 20),
        name="input_grad",
    )(core, theirs, mine, weights)


def shrink(value):
    taps = value.shape[1]
    power, count = exponent(jnp.max(jnp.abs(value), axis=(1, 3), keepdims=True))
    wide = jnp.pad(value, ((0, 0), (0, 1), (0, 0), (0, 0)))
    tap = lax.broadcasted_iota(jnp.int32, wide.shape, 1)
    return jnp.where(tap < taps, wide * power, count).astype(F16)


def grow(packed):
    taps = packed.shape[1] - 1
    power = inverse(packed[:, taps:, :, :1].astype(F32))
    return packed[:, :taps].astype(F32) * power


def on_device(inputs, kernel, cotangent):
    height, width, local_in = inputs.shape[1:]
    channels = kernel.shape[3]
    groups = lax.axis_size("filter")
    chips = lax.axis_size("chip")
    samples = chips * lax.axis_size("core")
    share = channels // samples
    cells = height * width
    x = inputs.reshape(cells, local_in)
    weights = kernel.reshape(9 * local_in, channels)
    rows = cells // groups
    cot = cotangent.reshape(rows, channels)
    core = lax.axis_index("core").astype(jnp.int32).reshape(1)
    scale = 1.0 / float(samples * cells) ** 0.5

    both = split_by_core(core, cot, share)
    partial = forward_partial(width, x, weights)
    summed = lax.psum_scatter(partial, "filter", scatter_dimension=0, tiled=True)
    outputs = summed.astype(BF16).reshape(cotangent.shape)
    gathered = lax.all_gather(both.astype(F16), "filter", axis=0).astype(BF16)
    theirs_grad, theirs_turned, mine_whole, patches = weight_first(
        width, scale, share, x, gathered
    )
    received = lax.ppermute(theirs_grad, "core", [(0, 1), (1, 0)])
    mine_grad, mine_turned = weight_second(scale, share, mine_whole, patches)
    packed = shrink(mine_grad + received)
    input_grad = input_gradient(width, share, core, theirs_turned, mine_turned, weights)
    input_grad = input_grad.reshape(inputs.shape)

    packed = lax.all_to_all(packed, "chip", 0, 0, tiled=True)
    kernel_grad = jnp.sum(grow(packed), axis=0).transpose(1, 0, 2)
    return (outputs, input_grad, kernel_grad.reshape(share, 3, 3, local_in))


def solution(mesh):
    samples, groups = mesh.devices.shape
    split = Mesh(
        mesh.devices.reshape(samples // 2, 2, groups), ("chip", "core", "filter")
    )
    dp = ("chip", "core")
    return jax.shard_map(
        on_device,
        mesh=split,
        in_specs=(
            P(dp, None, None, "filter"),
            P(None, None, "filter", None),
            P(dp, "filter", None, None),
        ),
        out_specs=(
            P(dp, "filter", None, None),
            P(dp, None, None, "filter"),
            P(dp, None, None, "filter"),
        ),
        check_vma=False,
    )
```

```python
import functools

import jax
import jax.numpy as jnp
from jax import lax
from jax.experimental import pallas as pl
from jax.experimental.pallas import tpu as pltpu
from jax.sharding import Mesh, PartitionSpec as P

F32 = jnp.float32
BF16 = jnp.bfloat16
F16 = jnp.float16
STEPS = (64, 32, 16, 8, 4, 2, 1)


def build_patches(width, x_ref, pad_ref, patch_ref):
    cells, chans = x_ref.shape
    value = x_ref[...].astype(F32)
    column = lax.rem(lax.broadcasted_iota(jnp.int32, value.shape, 0), width)
    left = jnp.where(column == 0, 0.0, pltpu.roll(value, 1, 0))
    right = jnp.where(column == width - 1, 0.0, pltpu.roll(value, cells - 1, 0))
    for b, shifted in enumerate((left, value, right)):
        pad_ref[b, :width, :] = jnp.zeros((width, chans), BF16)
        pad_ref[b, width : width + cells, :] = shifted.astype(BF16)
        pad_ref[b, width + cells :, :] = jnp.zeros((width, chans), BF16)
    for a in range(3):
        for b in range(3):
            tap = 3 * a + b
            patch_ref[:, tap * chans : (tap + 1) * chans] = pad_ref[
                b, a * width : a * width + cells, :
            ]


def exponent(top):
    power = jnp.ones_like(top)
    count = jnp.zeros_like(top)
    for step in STEPS:
        fits = top * (2.0**step) < 32768.0
        factor = jnp.where(fits, 2.0**step, 1.0)
        top = top * factor
        power = power * factor
        count = count + jnp.where(fits, float(step), 0.0)
    return power, count


def inverse(count):
    power = jnp.ones_like(count)
    for step in STEPS:
        has = count >= step
        power = power * jnp.where(has, 2.0**-step, 1.0)
        count = count - jnp.where(has, float(step), 0.0)
    return power


def split_by_core(share, core, cot_ref, out_ref):
    rows, channels = cot_ref.shape
    half = channels // 2
    source = lax.broadcasted_iota(jnp.int32, (channels, half), 0)
    target = lax.broadcasted_iota(jnp.int32, (channels, half), 1)
    place = (target // share) * (2 * share) + lax.rem(target, share)
    top = jnp.max(jnp.abs(cot_ref[...].astype(F32)), axis=0, keepdims=True)
    top = jnp.max(top, axis=1, keepdims=True)
    power, count = exponent(jnp.broadcast_to(top, (8, half)))
    for slot, owner in ((0, 1 - core), (1, core)):
        pick = jnp.where(source == place + owner * share, 1.0, 0.0).astype(BF16)
        value = jnp.dot(cot_ref[...], pick, preferred_element_type=F32)
        out_ref[slot * rows : (slot + 1) * rows, :] = value * power[:1]
    out_ref[2 * rows :, :] = count


def forward_kernel(width, share, core_ref, x_ref, cot_ref, kernel_ref, *refs):
    out_ref, both_ref, patch_ref, pad_ref = refs

    @pl.when(pl.program_id(0) == 0)
    def _():
        build_patches(width, x_ref, pad_ref, patch_ref)
        split_by_core(share, core_ref[0], cot_ref, both_ref)

    out_ref[...] = jnp.dot(patch_ref[...], kernel_ref[...], preferred_element_type=F32)


def forward_partial(width, share, core, x, cot, weights):
    cells, chans = x.shape
    taps, channels = weights.shape
    rows = 2 * cot.shape[0] + 8
    block = channels // 4
    x = pltpu.with_memory_space_constraint(x, pltpu.HBM)
    cot = pltpu.with_memory_space_constraint(cot, pltpu.HBM)
    weights = pltpu.with_memory_space_constraint(weights, pltpu.HBM)
    return pl.pallas_call(
        functools.partial(forward_kernel, width, share),
        out_shape=(
            pltpu.HBM((cells, channels), F32),
            jax.ShapeDtypeStruct((rows, channels // 2), F32),
            jax.ShapeDtypeStruct((cells, taps), BF16),
        ),
        grid=(4,),
        in_specs=[
            pl.BlockSpec(memory_space=pltpu.SMEM),
            pl.BlockSpec((cells, chans), lambda i: (0, 0)),
            pl.BlockSpec(cot.shape, lambda i: (0, 0)),
            pl.BlockSpec((taps, block), lambda i: (0, i)),
        ],
        out_specs=(
            pl.BlockSpec((cells, block), lambda i: (0, i)),
            pl.BlockSpec((rows, channels // 2), lambda i: (0, 0)),
            pl.BlockSpec((cells, taps), lambda i: (0, 0)),
        ),
        scratch_shapes=[pltpu.VMEM((3, cells + 2 * width, chans), BF16)],
        compiler_params=pltpu.CompilerParams(vmem_limit_bytes=24 << 20),
        name="forward",
    )(core, x, cot, weights)


def multiply_turned(scale, cot_ref, patch_ref, grad_ref, turned_ref):
    turned = cot_ref[...].T
    turned_ref[...] = turned
    grad = scale * jnp.dot(turned, patch_ref[...], preferred_element_type=F32)
    chips, rows, chans = grad_ref.shape
    share = rows // 9
    for chip in range(chips):
        for tap in range(9):
            grad_ref[chip, tap * share : (tap + 1) * share, :] = grad[
                chip * share : (chip + 1) * share, tap * chans : (tap + 1) * chans
            ]


def first_kernel(scale, patch_ref, all_ref, grad_ref, turned_ref, mine_ref, cot_ref):
    groups = all_ref.shape[0]
    rows = (all_ref.shape[1] - 8) // 2
    for group in range(groups):
        power = inverse(all_ref[group, 2 * rows :, :].astype(F32))[:1]
        for slot, ref in ((0, cot_ref), (1, mine_ref)):
            value = all_ref[group, slot * rows : (slot + 1) * rows, :].astype(F32) * power
            ref[group * rows : (group + 1) * rows, :] = value.astype(BF16)
    multiply_turned(scale, cot_ref, patch_ref, grad_ref, turned_ref)


def weight_first(scale, share, patches, gathered):
    cells = patches.shape[0]
    chans = patches.shape[1] // 9
    half = gathered.shape[2]
    vmem = pl.BlockSpec(memory_space=pltpu.VMEM)
    return pl.pallas_call(
        functools.partial(first_kernel, scale),
        out_shape=(
            jax.ShapeDtypeStruct((half // share, 9 * share, chans), F32),
            jax.ShapeDtypeStruct((half, cells), BF16),
            jax.ShapeDtypeStruct((cells, half), BF16),
        ),
        in_specs=[vmem, vmem],
        out_specs=(vmem,) * 3,
        scratch_shapes=[pltpu.VMEM((cells, half), BF16)],
        compiler_params=pltpu.CompilerParams(vmem_limit_bytes=24 << 20),
        name="weight_first",
    )(patches, gathered)


def second_kernel(scale, cot_ref, patch_ref, grad_ref, turned_ref):
    multiply_turned(scale, cot_ref, patch_ref, grad_ref, turned_ref)


def weight_second(scale, share, cot, patches):
    cells, half = cot.shape
    chans = patches.shape[1] // 9
    vmem = pl.BlockSpec(memory_space=pltpu.VMEM)
    return pl.pallas_call(
        functools.partial(second_kernel, scale),
        out_shape=(
            jax.ShapeDtypeStruct((half // share, 9 * share, chans), F32),
            jax.ShapeDtypeStruct((half, cells), BF16),
        ),
        in_specs=[vmem, vmem],
        out_specs=(vmem, vmem),
        compiler_params=pltpu.CompilerParams(vmem_limit_bytes=24 << 20),
        name="weight_second",
    )(cot, patches)


def input_kernel(width, share, core_ref, theirs_ref, mine_ref, kernel_ref, out_ref, cot_ref):
    cells, chans = out_ref.shape
    chips = theirs_ref.shape[0] // share
    core = core_ref[0]
    for ref, owner in ((theirs_ref, 1 - core), (mine_ref, core)):
        for chip in range(chips):
            start = pl.multiple_of((2 * chip + owner) * share, share)
            cot_ref[pl.ds(start, share), :] = ref[chip * share : (chip + 1) * share, :]
    spread = jnp.dot(kernel_ref[...], cot_ref[...], preferred_element_type=F32)
    cell = lax.broadcasted_iota(jnp.int32, (chans, cells), 1)
    column = lax.rem(cell, width)
    total = None
    for b in range(3):
        part = None
        for a in range(3):
            tap = 3 * a + b
            term = spread[tap * chans : (tap + 1) * chans, :]
            if a == 0:
                term = jnp.where(cell < cells - width, pltpu.roll(term, cells - width, 1), 0.0)
            if a == 2:
                term = jnp.where(cell >= width, pltpu.roll(term, width, 1), 0.0)
            part = term if part is None else part + term
        if b == 0:
            part = jnp.where(column < width - 1, pltpu.roll(part, cells - 1, 1), 0.0)
        if b == 2:
            part = jnp.where(column > 0, pltpu.roll(part, 1, 1), 0.0)
        total = part if total is None else total + part
    out_ref[...] = total.T.astype(BF16)


def input_gradient(width, share, core, theirs, mine, weights):
    cells = theirs.shape[1]
    chans = weights.shape[0] // 9
    vmem = pl.BlockSpec(memory_space=pltpu.VMEM)
    return pl.pallas_call(
        functools.partial(input_kernel, width, share),
        out_shape=jax.ShapeDtypeStruct((cells, chans), BF16),
        in_specs=[pl.BlockSpec(memory_space=pltpu.SMEM)] + [vmem] * 3,
        out_specs=vmem,
        scratch_shapes=[pltpu.VMEM((weights.shape[1], cells), BF16)],
        compiler_params=pltpu.CompilerParams(vmem_limit_bytes=24 << 20),
        name="input_grad",
    )(core, theirs, mine, weights)


def shrink(value):
    rows = value.shape[1]
    power, count = exponent(jnp.max(jnp.abs(value), axis=(1, 2), keepdims=True))
    wide = jnp.pad(value, ((0, 0), (0, 8), (0, 0)))
    row = lax.broadcasted_iota(jnp.int32, wide.shape, 1)
    return jnp.where(row < rows, wide * power, count).astype(F16)


def grow(packed):
    power = inverse(packed[:, -8:-7, :1].astype(F32))
    return packed[:, :-8].astype(F32) * power


def on_device(inputs, kernel, cotangent):
    height, width, local_in = inputs.shape[1:]
    channels = kernel.shape[3]
    groups = lax.axis_size("filter")
    chips = lax.axis_size("chip")
    samples = chips * lax.axis_size("core")
    share = channels // samples
    cells = height * width
    x = inputs.reshape(cells, local_in)
    weights = kernel.reshape(9 * local_in, channels)
    rows = cells // groups
    cot = cotangent.reshape(rows, channels)
    core = lax.axis_index("core").astype(jnp.int32).reshape(1)
    scale = 1.0 / float(samples * cells) ** 0.5

    partial, both, patches = forward_partial(width, share, core, x, cot, weights)
    summed = lax.psum_scatter(partial, "filter", scatter_dimension=0, tiled=True)
    outputs = summed.astype(BF16).reshape(cotangent.shape)
    gathered = lax.all_gather(both.astype(F16), "filter", axis=0).astype(BF16)
    theirs_grad, theirs_turned, mine_whole = weight_first(scale, share, patches, gathered)
    received = lax.ppermute(theirs_grad, "core", [(0, 1), (1, 0)])
    mine_grad, mine_turned = weight_second(scale, share, mine_whole, patches)
    packed = shrink(mine_grad + received)
    input_grad = input_gradient(width, share, core, theirs_turned, mine_turned, weights)
    input_grad = input_grad.reshape(inputs.shape)

    packed = lax.all_to_all(packed, "chip", 0, 0, tiled=True)
    packed, outputs = lax.optimization_barrier((packed, outputs))
    kernel_grad = jnp.sum(grow(packed), axis=0).reshape(9, share, local_in)
    kernel_grad = kernel_grad.transpose(1, 0, 2)
    return (outputs, input_grad, kernel_grad.reshape(share, 3, 3, local_in))


def solution(mesh):
    samples, groups = mesh.devices.shape
    split = Mesh(
        mesh.devices.reshape(samples // 2, 2, groups), ("chip", "core", "filter")
    )
    dp = ("chip", "core")
    return jax.shard_map(
        on_device,
        mesh=split,
        in_specs=(
            P(dp, None, None, "filter"),
            P(None, None, "filter", None),
            P(dp, "filter", None, None),
        ),
        out_specs=(
            P(dp, "filter", None, None),
            P(dp, None, None, "filter"),
            P(dp, None, None, "filter"),
        ),
        check_vma=False,
    )
```

```python
import functools

import jax
import jax.numpy as jnp
from jax import lax
from jax.experimental import pallas as pl
from jax.experimental.pallas import tpu as pltpu
from jax.sharding import Mesh, PartitionSpec as P

F32 = jnp.float32
BF16 = jnp.bfloat16
F16 = jnp.float16
STEPS = (64, 32, 16, 8, 4, 2, 1)


def build_patches(width, x_ref, pad_ref, patch_ref):
    cells, chans = x_ref.shape
    value = x_ref[...].astype(F32)
    column = lax.rem(lax.broadcasted_iota(jnp.int32, value.shape, 0), width)
    left = jnp.where(column == 0, 0.0, pltpu.roll(value, 1, 0))
    right = jnp.where(column == width - 1, 0.0, pltpu.roll(value, cells - 1, 0))
    for b, shifted in enumerate((left, value, right)):
        pad_ref[b, :width, :] = jnp.zeros((width, chans), BF16)
        pad_ref[b, width : width + cells, :] = shifted.astype(BF16)
        pad_ref[b, width + cells :, :] = jnp.zeros((width, chans), BF16)
    for a in range(3):
        for b in range(3):
            tap = 3 * a + b
            patch_ref[:, tap * chans : (tap + 1) * chans] = pad_ref[
                b, a * width : a * width + cells, :
            ]


def exponent(top):
    power = jnp.ones_like(top)
    count = jnp.zeros_like(top)
    for step in STEPS:
        fits = top * (2.0**step) < 32768.0
        factor = jnp.where(fits, 2.0**step, 1.0)
        top = top * factor
        power = power * factor
        count = count + jnp.where(fits, float(step), 0.0)
    return power, count


def inverse(count):
    power = jnp.ones_like(count)
    for step in STEPS:
        has = count >= step
        power = power * jnp.where(has, 2.0**-step, 1.0)
        count = count - jnp.where(has, float(step), 0.0)
    return power


def split_by_core(share, core, cot_ref, out_ref):
    rows, channels = cot_ref.shape
    half = channels // 2
    source = lax.broadcasted_iota(jnp.int32, (256, 128), 0)
    target = lax.broadcasted_iota(jnp.int32, (256, 128), 1)
    place = (target // share) * (2 * share) + lax.rem(target, share)
    top = jnp.max(jnp.abs(cot_ref[...].astype(F32)), axis=0, keepdims=True)
    top = jnp.max(top, axis=1, keepdims=True)
    power, count = exponent(jnp.broadcast_to(top, (8, half)))
    for slot, owner in ((0, 1 - core), (1, core)):
        pick = jnp.where(source == place + owner * share, 1.0, 0.0).astype(BF16)
        for k in range(half // 128):
            value = jnp.dot(
                cot_ref[:, 256 * k : 256 * (k + 1)], pick, preferred_element_type=F32
            )
            out_ref[slot * rows : (slot + 1) * rows, 128 * k : 128 * (k + 1)] = (
                value * power[:1, :128]
            )
    out_ref[2 * rows :, :] = count


def forward_kernel(width, share, core_ref, x_ref, cot_ref, kernel_ref, *refs):
    out_ref, both_ref, patch_ref, pad_ref = refs

    @pl.when(pl.program_id(0) == 0)
    def _():
        build_patches(width, x_ref, pad_ref, patch_ref)
        split_by_core(share, core_ref[0], cot_ref, both_ref)

    out_ref[...] = jnp.dot(patch_ref[...], kernel_ref[...], preferred_element_type=F32)


def forward_partial(width, share, core, x, cot, weights):
    cells, chans = x.shape
    taps, channels = weights.shape
    rows = 2 * cot.shape[0] + 8
    block = channels // 4
    x = pltpu.with_memory_space_constraint(x, pltpu.HBM)
    cot = pltpu.with_memory_space_constraint(cot, pltpu.HBM)
    weights = pltpu.with_memory_space_constraint(weights, pltpu.HBM)
    return pl.pallas_call(
        functools.partial(forward_kernel, width, share),
        out_shape=(
            pltpu.HBM((cells, channels), F32),
            jax.ShapeDtypeStruct((rows, channels // 2), F32),
            jax.ShapeDtypeStruct((cells, taps), BF16),
        ),
        grid=(4,),
        in_specs=[
            pl.BlockSpec(memory_space=pltpu.SMEM),
            pl.BlockSpec((cells, chans), lambda i: (0, 0)),
            pl.BlockSpec(cot.shape, lambda i: (0, 0)),
            pl.BlockSpec((taps, block), lambda i: (0, i)),
        ],
        out_specs=(
            pl.BlockSpec((cells, block), lambda i: (0, i)),
            pl.BlockSpec((rows, channels // 2), lambda i: (0, 0)),
            pl.BlockSpec((cells, taps), lambda i: (0, 0)),
        ),
        scratch_shapes=[pltpu.VMEM((3, cells + 2 * width, chans), BF16)],
        compiler_params=pltpu.CompilerParams(vmem_limit_bytes=24 << 20),
        name="forward",
    )(core, x, cot, weights)


def multiply_turned(scale, cot, patch_ref, grad_ref, turned_ref):
    turned = cot.T
    turned_ref[...] = turned
    grad = scale * jnp.dot(turned, patch_ref[...], preferred_element_type=F32)
    chips, rows, chans = grad_ref.shape
    share = rows // 9
    for chip in range(chips):
        for tap in range(9):
            grad_ref[chip, tap * share : (tap + 1) * share, :] = grad[
                chip * share : (chip + 1) * share, tap * chans : (tap + 1) * chans
            ]


def first_kernel(scale, patch_ref, all_ref, grad_ref, turned_ref, cot_ref, mine_ref):
    groups = all_ref.shape[0]
    rows = (all_ref.shape[1] - 8) // 2
    for group in range(groups):
        power = inverse(all_ref[group, 2 * rows :, :].astype(F32))[:1]
        for slot, ref in ((0, cot_ref), (1, mine_ref)):
            value = all_ref[group, slot * rows : (slot + 1) * rows, :].astype(F32) * power
            ref[group * rows : (group + 1) * rows, :] = value.astype(BF16)
    start = cot_ref[:, : turned_ref.shape[0]]
    multiply_turned(scale, start, patch_ref, grad_ref, turned_ref)


def weight_first(scale, share, patches, gathered):
    cells = patches.shape[0]
    chans = patches.shape[1] // 9
    half = gathered.shape[2]
    vmem = pl.BlockSpec(memory_space=pltpu.VMEM)
    return pl.pallas_call(
        functools.partial(first_kernel, scale),
        out_shape=(
            jax.ShapeDtypeStruct((half // 2 // share, 9 * share, chans), F32),
            pltpu.HBM((half // 2, cells), BF16),
            jax.ShapeDtypeStruct((cells, half), BF16),
            jax.ShapeDtypeStruct((cells, half), BF16),
        ),
        in_specs=[vmem, vmem],
        out_specs=(vmem,) * 4,
        compiler_params=pltpu.CompilerParams(vmem_limit_bytes=24 << 20),
        name="weight_first",
    )(patches, gathered)


def second_kernel(scale, cot_ref, patch_ref, grad_ref, turned_ref):
    multiply_turned(scale, cot_ref[...], patch_ref, grad_ref, turned_ref)


def weight_second(scale, share, cot, patches, parts, part):
    cells = cot.shape[0]
    half = cot.shape[1] // parts
    chans = patches.shape[1] // 9
    vmem = pl.BlockSpec(memory_space=pltpu.VMEM)
    return pl.pallas_call(
        functools.partial(second_kernel, scale),
        out_shape=(
            jax.ShapeDtypeStruct((half // share, 9 * share, chans), F32),
            pltpu.HBM((half, cells), BF16),
        ),
        grid=(1,),
        in_specs=[pl.BlockSpec((cells, half), lambda i: (0, part)), vmem],
        out_specs=(vmem, vmem),
        compiler_params=pltpu.CompilerParams(vmem_limit_bytes=24 << 20),
        name="weight_second",
    )(cot, patches)


def input_kernel(width, share, core_ref, *refs):
    early_ref, late_ref, mine_ref, kernel_ref, out_ref, cot_ref = refs
    cells, chans = out_ref.shape
    core = core_ref[0]
    middle = early_ref.shape[0] // share
    for ref, owner, first in (
        (early_ref, 1 - core, 0),
        (late_ref, 1 - core, middle),
        (mine_ref, core, 0),
    ):
        for chip in range(ref.shape[0] // share):
            start = pl.multiple_of((2 * (first + chip) + owner) * share, share)
            cot_ref[pl.ds(start, share), :] = ref[chip * share : (chip + 1) * share, :]
    spread = jnp.dot(kernel_ref[...], cot_ref[...], preferred_element_type=F32)
    cell = lax.broadcasted_iota(jnp.int32, (chans, cells), 1)
    column = lax.rem(cell, width)
    total = None
    for b in range(3):
        part = None
        for a in range(3):
            tap = 3 * a + b
            term = spread[tap * chans : (tap + 1) * chans, :]
            if a == 0:
                term = jnp.where(cell < cells - width, pltpu.roll(term, cells - width, 1), 0.0)
            if a == 2:
                term = jnp.where(cell >= width, pltpu.roll(term, width, 1), 0.0)
            part = term if part is None else part + term
        if b == 0:
            part = jnp.where(column < width - 1, pltpu.roll(part, cells - 1, 1), 0.0)
        if b == 2:
            part = jnp.where(column > 0, pltpu.roll(part, 1, 1), 0.0)
        total = part if total is None else total + part
    out_ref[...] = total.T.astype(BF16)


def input_gradient(width, share, core, early, late, mine, weights):
    cells = mine.shape[1]
    chans = weights.shape[0] // 9
    vmem = pl.BlockSpec(memory_space=pltpu.VMEM)
    return pl.pallas_call(
        functools.partial(input_kernel, width, share),
        out_shape=jax.ShapeDtypeStruct((cells, chans), BF16),
        in_specs=[pl.BlockSpec(memory_space=pltpu.SMEM)] + [vmem] * 4,
        out_specs=vmem,
        scratch_shapes=[pltpu.VMEM((weights.shape[1], cells), BF16)],
        compiler_params=pltpu.CompilerParams(vmem_limit_bytes=24 << 20),
        name="input_grad",
    )(core, early, late, mine, weights)


def shrink(value):
    rows = value.shape[1]
    power, count = exponent(jnp.max(jnp.abs(value), axis=(1, 2), keepdims=True))
    wide = jnp.pad(value, ((0, 0), (0, 8), (0, 0)))
    row = lax.broadcasted_iota(jnp.int32, wide.shape, 1)
    return jnp.where(row < rows, wide * power, count).astype(F16)


def grow(packed):
    power = inverse(packed[:, -8:-7, :].astype(F32))
    return packed[:, :-8].astype(F32) * power


def on_device(inputs, kernel, cotangent):
    height, width, local_in = inputs.shape[1:]
    channels = kernel.shape[3]
    groups = lax.axis_size("filter")
    chips = lax.axis_size("chip")
    samples = chips * lax.axis_size("core")
    share = channels // samples
    cells = height * width
    x = inputs.reshape(cells, local_in)
    weights = kernel.reshape(9 * local_in, channels)
    rows = cells // groups
    cot = cotangent.reshape(rows, channels)
    core = lax.axis_index("core").astype(jnp.int32).reshape(1)
    scale = 1.0 / float(samples * cells) ** 0.5

    partial, both, patches = forward_partial(width, share, core, x, cot, weights)
    summed = lax.psum_scatter(partial, "filter", scatter_dimension=0, tiled=True)
    outputs = summed.astype(BF16).reshape(cotangent.shape)
    gathered = lax.all_gather(both.astype(F16), "filter", axis=0).astype(BF16)
    swap = [(0, 1), (1, 0)]
    early, early_turned, theirs, mine = weight_first(scale, share, patches, gathered)
    early = lax.ppermute(early, "core", swap)
    late, late_turned = weight_second(scale, share, theirs, patches, 2, 1)
    late = lax.ppermute(late, "core", swap)
    mine_grad, mine_turned = weight_second(scale, share, mine, patches, 1, 0)
    packed = shrink(mine_grad + jnp.concatenate([early, late], axis=0))
    input_grad = input_gradient(
        width, share, core, early_turned, late_turned, mine_turned, weights
    )
    input_grad = input_grad.reshape(inputs.shape)

    packed = lax.all_to_all(packed, "chip", 0, 0, tiled=True)
    packed, outputs = lax.optimization_barrier((packed, outputs))
    kernel_grad = jnp.sum(grow(packed), axis=0).reshape(9, share, local_in)
    kernel_grad = kernel_grad.transpose(1, 0, 2)
    return (outputs, input_grad, kernel_grad.reshape(share, 3, 3, local_in))


def solution(mesh):
    samples, groups = mesh.devices.shape
    split = Mesh(
        mesh.devices.reshape(samples // 2, 2, groups), ("chip", "core", "filter")
    )
    dp = ("chip", "core")
    return jax.shard_map(
        on_device,
        mesh=split,
        in_specs=(
            P(dp, None, None, "filter"),
            P(None, None, "filter", None),
            P(dp, "filter", None, None),
        ),
        out_specs=(
            P(dp, "filter", None, None),
            P(dp, None, None, "filter"),
            P(dp, None, None, "filter"),
        ),
        check_vma=False,
    )
```

```python
import functools

import jax
import jax.numpy as jnp
from jax import lax
from jax.experimental import pallas as pl
from jax.experimental.pallas import tpu as pltpu
from jax.sharding import Mesh, PartitionSpec as P

F32 = jnp.float32
BF16 = jnp.bfloat16
F16 = jnp.float16
STEPS = (64, 32, 16, 8, 4, 2, 1)


def build_patches(width, x_ref, pad_ref, patch_ref):
    cells, chans = x_ref.shape
    value = x_ref[...].astype(F32)
    column = lax.rem(lax.broadcasted_iota(jnp.int32, value.shape, 0), width)
    left = jnp.where(column == 0, 0.0, pltpu.roll(value, 1, 0))
    right = jnp.where(column == width - 1, 0.0, pltpu.roll(value, cells - 1, 0))
    for b, shifted in enumerate((left, value, right)):
        pad_ref[b, :width, :] = jnp.zeros((width, chans), BF16)
        pad_ref[b, width : width + cells, :] = shifted.astype(BF16)
        pad_ref[b, width + cells :, :] = jnp.zeros((width, chans), BF16)
    for a in range(3):
        for b in range(3):
            tap = 3 * a + b
            patch_ref[:, tap * chans : (tap + 1) * chans] = pad_ref[
                b, a * width : a * width + cells, :
            ]


def exponent(top):
    power = jnp.ones_like(top)
    count = jnp.zeros_like(top)
    for step in STEPS:
        fits = top * (2.0**step) < 32768.0
        factor = jnp.where(fits, 2.0**step, 1.0)
        top = top * factor
        power = power * factor
        count = count + jnp.where(fits, float(step), 0.0)
    return power, count


def inverse(count):
    power = jnp.ones_like(count)
    for step in STEPS:
        has = count >= step
        power = power * jnp.where(has, 2.0**-step, 1.0)
        count = count - jnp.where(has, float(step), 0.0)
    return power


def split_by_core(share, core, cot_ref, out_ref):
    rows, channels = cot_ref.shape
    half = channels // 2
    source = lax.broadcasted_iota(jnp.int32, (256, 128), 0)
    target = lax.broadcasted_iota(jnp.int32, (256, 128), 1)
    place = (target // share) * (2 * share) + lax.rem(target, share)
    top = jnp.max(jnp.abs(cot_ref[...].astype(F32)), axis=0, keepdims=True)
    top = jnp.max(top, axis=1, keepdims=True)
    power, count = exponent(jnp.broadcast_to(top, (8, half)))
    for slot, owner in ((0, 1 - core), (1, core)):
        pick = jnp.where(source == place + owner * share, 1.0, 0.0).astype(BF16)
        for k in range(half // 128):
            value = jnp.dot(
                cot_ref[:, 256 * k : 256 * (k + 1)], pick, preferred_element_type=F32
            )
            out_ref[slot * rows : (slot + 1) * rows, 128 * k : 128 * (k + 1)] = (
                value * power[:1, :128]
            )
    out_ref[2 * rows :, :] = count


def forward_kernel(width, share, core_ref, x_ref, cot_ref, kernel_ref, *refs):
    out_ref, both_ref, patch_ref, pad_ref = refs

    @pl.when(pl.program_id(0) == 0)
    def _():
        build_patches(width, x_ref, pad_ref, patch_ref)
        split_by_core(share, core_ref[0], cot_ref, both_ref)

    out_ref[...] = jnp.dot(patch_ref[...], kernel_ref[...], preferred_element_type=F32)


def forward_partial(width, share, core, x, cot, weights):
    cells, chans = x.shape
    taps, channels = weights.shape
    rows = 2 * cot.shape[0] + 8
    block = channels // 2
    x = pltpu.with_memory_space_constraint(x, pltpu.HBM)
    cot = pltpu.with_memory_space_constraint(cot, pltpu.HBM)
    weights = pltpu.with_memory_space_constraint(weights, pltpu.HBM)
    return pl.pallas_call(
        functools.partial(forward_kernel, width, share),
        out_shape=(
            pltpu.HBM((cells, channels), F32),
            jax.ShapeDtypeStruct((rows, channels // 2), F32),
            jax.ShapeDtypeStruct((cells, taps), BF16),
        ),
        grid=(2,),
        in_specs=[
            pl.BlockSpec(memory_space=pltpu.SMEM),
            pl.BlockSpec((cells, chans), lambda i: (0, 0)),
            pl.BlockSpec(cot.shape, lambda i: (0, 0)),
            pl.BlockSpec((taps, block), lambda i: (0, i)),
        ],
        out_specs=(
            pl.BlockSpec((cells, block), lambda i: (0, i)),
            pl.BlockSpec((rows, channels // 2), lambda i: (0, 0)),
            pl.BlockSpec((cells, taps), lambda i: (0, 0)),
        ),
        scratch_shapes=[pltpu.VMEM((3, cells + 2 * width, chans), BF16)],
        compiler_params=pltpu.CompilerParams(vmem_limit_bytes=24 << 20),
        name="forward",
    )(core, x, cot, weights)


def multiply_turned(scale, cot, patch_ref, grad_ref, turned_ref):
    turned = cot.T
    turned_ref[...] = turned
    grad = scale * jnp.dot(turned, patch_ref[...], preferred_element_type=F32)
    chips, rows, chans = grad_ref.shape
    share = rows // 9
    for chip in range(chips):
        for tap in range(9):
            grad_ref[chip, tap * share : (tap + 1) * share, :] = grad[
                chip * share : (chip + 1) * share, tap * chans : (tap + 1) * chans
            ]


def first_kernel(scale, patch_ref, all_ref, grad_ref, turned_ref, cot_ref, mine_ref):
    groups = all_ref.shape[0]
    rows = (all_ref.shape[1] - 8) // 2
    for group in range(groups):
        power = inverse(all_ref[group, 2 * rows :, :].astype(F32))[:1]
        for slot, ref in ((0, cot_ref), (1, mine_ref)):
            value = all_ref[group, slot * rows : (slot + 1) * rows, :].astype(F32) * power
            ref[group * rows : (group + 1) * rows, :] = value.astype(BF16)
    start = cot_ref[:, : turned_ref.shape[0]]
    multiply_turned(scale, start, patch_ref, grad_ref, turned_ref)


def weight_first(scale, share, patches, gathered):
    cells = patches.shape[0]
    chans = patches.shape[1] // 9
    half = gathered.shape[2]
    vmem = pl.BlockSpec(memory_space=pltpu.VMEM)
    return pl.pallas_call(
        functools.partial(first_kernel, scale),
        out_shape=(
            jax.ShapeDtypeStruct((half // 2 // share, 9 * share, chans), F32),
            pltpu.HBM((half // 2, cells), BF16),
            jax.ShapeDtypeStruct((cells, half), BF16),
            jax.ShapeDtypeStruct((cells, half), BF16),
        ),
        in_specs=[vmem, vmem],
        out_specs=(vmem,) * 4,
        compiler_params=pltpu.CompilerParams(vmem_limit_bytes=24 << 20),
        name="weight_first",
    )(patches, gathered)


def second_kernel(scale, cot_ref, patch_ref, grad_ref, turned_ref):
    multiply_turned(scale, cot_ref[...], patch_ref, grad_ref, turned_ref)


def weight_second(scale, share, cot, patches, parts, part):
    cells = cot.shape[0]
    half = cot.shape[1] // parts
    chans = patches.shape[1] // 9
    vmem = pl.BlockSpec(memory_space=pltpu.VMEM)
    return pl.pallas_call(
        functools.partial(second_kernel, scale),
        out_shape=(
            jax.ShapeDtypeStruct((half // share, 9 * share, chans), F32),
            pltpu.HBM((half, cells), BF16),
        ),
        grid=(1,),
        in_specs=[pl.BlockSpec((cells, half), lambda i: (0, part)), vmem],
        out_specs=(vmem, vmem),
        compiler_params=pltpu.CompilerParams(vmem_limit_bytes=24 << 20),
        name="weight_second",
    )(cot, patches)


def input_kernel(width, share, core_ref, *refs):
    early_ref, late_ref, mine_ref, kernel_ref, out_ref, cot_ref = refs
    cells, chans = out_ref.shape
    core = core_ref[0]
    middle = early_ref.shape[0] // share
    for ref, owner, first in (
        (early_ref, 1 - core, 0),
        (late_ref, 1 - core, middle),
        (mine_ref, core, 0),
    ):
        for chip in range(ref.shape[0] // share):
            start = pl.multiple_of((2 * (first + chip) + owner) * share, share)
            cot_ref[pl.ds(start, share), :] = ref[chip * share : (chip + 1) * share, :]
    spread = jnp.dot(kernel_ref[...], cot_ref[...], preferred_element_type=F32)
    cell = lax.broadcasted_iota(jnp.int32, (chans, cells), 1)
    column = lax.rem(cell, width)
    total = None
    for b in range(3):
        part = None
        for a in range(3):
            tap = 3 * a + b
            term = spread[tap * chans : (tap + 1) * chans, :]
            if a == 0:
                term = jnp.where(cell < cells - width, pltpu.roll(term, cells - width, 1), 0.0)
            if a == 2:
                term = jnp.where(cell >= width, pltpu.roll(term, width, 1), 0.0)
            part = term if part is None else part + term
        if b == 0:
            part = jnp.where(column < width - 1, pltpu.roll(part, cells - 1, 1), 0.0)
        if b == 2:
            part = jnp.where(column > 0, pltpu.roll(part, 1, 1), 0.0)
        total = part if total is None else total + part
    out_ref[...] = total.T.astype(BF16)


def input_gradient(width, share, core, early, late, mine, weights):
    cells = mine.shape[1]
    chans = weights.shape[0] // 9
    vmem = pl.BlockSpec(memory_space=pltpu.VMEM)
    return pl.pallas_call(
        functools.partial(input_kernel, width, share),
        out_shape=jax.ShapeDtypeStruct((cells, chans), BF16),
        in_specs=[pl.BlockSpec(memory_space=pltpu.SMEM)] + [vmem] * 4,
        out_specs=vmem,
        scratch_shapes=[pltpu.VMEM((weights.shape[1], cells), BF16)],
        compiler_params=pltpu.CompilerParams(vmem_limit_bytes=24 << 20),
        name="input_grad",
    )(core, early, late, mine, weights)


def shrink(value):
    rows = value.shape[1]
    power, count = exponent(jnp.max(jnp.abs(value), axis=(1, 2), keepdims=True))
    wide = jnp.pad(value, ((0, 0), (0, 8), (0, 0)))
    row = lax.broadcasted_iota(jnp.int32, wide.shape, 1)
    return jnp.where(row < rows, wide * power, count).astype(F16)


def grow(packed):
    power = inverse(packed[:, -8:-7, :].astype(F32))
    return packed[:, :-8].astype(F32) * power


def on_device(inputs, kernel, cotangent):
    height, width, local_in = inputs.shape[1:]
    channels = kernel.shape[3]
    groups = lax.axis_size("filter")
    chips = lax.axis_size("chip")
    samples = chips * lax.axis_size("core")
    share = channels // samples
    cells = height * width
    x = inputs.reshape(cells, local_in)
    weights = kernel.reshape(9 * local_in, channels)
    rows = cells // groups
    cot = cotangent.reshape(rows, channels)
    core = lax.axis_index("core").astype(jnp.int32).reshape(1)
    scale = 1.0 / float(samples * cells) ** 0.5

    partial, both, patches = forward_partial(width, share, core, x, cot, weights)
    summed = lax.psum_scatter(partial, "filter", scatter_dimension=0, tiled=True)
    outputs = summed.astype(BF16).reshape(cotangent.shape)
    gathered = lax.all_gather(both.astype(F16), "filter", axis=0).astype(BF16)
    swap = [(0, 1), (1, 0)]
    early, early_turned, theirs, mine = weight_first(scale, share, patches, gathered)
    early = lax.ppermute(early, "core", swap)
    late, late_turned = weight_second(scale, share, theirs, patches, 2, 1)
    late = lax.ppermute(late, "core", swap)
    mine_grad, mine_turned = weight_second(scale, share, mine, patches, 1, 0)
    packed = shrink(mine_grad + jnp.concatenate([early, late], axis=0))
    input_grad = input_gradient(
        width, share, core, early_turned, late_turned, mine_turned, weights
    )
    input_grad = input_grad.reshape(inputs.shape)

    packed = lax.all_to_all(packed, "chip", 0, 0, tiled=True)
    packed, outputs = lax.optimization_barrier((packed, outputs))
    kernel_grad = jnp.sum(grow(packed), axis=0).reshape(9, share, local_in)
    kernel_grad = kernel_grad.transpose(1, 0, 2)
    return (outputs, input_grad, kernel_grad.reshape(share, 3, 3, local_in))


def solution(mesh):
    samples, groups = mesh.devices.shape
    split = Mesh(
        mesh.devices.reshape(samples // 2, 2, groups), ("chip", "core", "filter")
    )
    dp = ("chip", "core")
    return jax.shard_map(
        on_device,
        mesh=split,
        in_specs=(
            P(dp, None, None, "filter"),
            P(None, None, "filter", None),
            P(dp, "filter", None, None),
        ),
        out_specs=(
            P(dp, "filter", None, None),
            P(dp, None, None, "filter"),
            P(dp, None, None, "filter"),
        ),
        check_vma=False,
    )
```

```python
import functools

import jax
import jax.numpy as jnp
from jax import lax
from jax.experimental import pallas as pl
from jax.experimental.pallas import tpu as pltpu
from jax.sharding import Mesh, PartitionSpec as P

F32 = jnp.float32
BF16 = jnp.bfloat16
F16 = jnp.float16
STEPS = (64, 32, 16, 8, 4, 2, 1)


def build_patches(width, x_ref, pad_ref, patch_ref):
    cells, chans = x_ref.shape
    value = x_ref[...].astype(F32)
    column = lax.rem(lax.broadcasted_iota(jnp.int32, value.shape, 0), width)
    left = jnp.where(column == 0, 0.0, pltpu.roll(value, 1, 0))
    right = jnp.where(column == width - 1, 0.0, pltpu.roll(value, cells - 1, 0))
    for b, shifted in enumerate((left, value, right)):
        pad_ref[b, :width, :] = jnp.zeros((width, chans), BF16)
        pad_ref[b, width : width + cells, :] = shifted.astype(BF16)
        pad_ref[b, width + cells :, :] = jnp.zeros((width, chans), BF16)
    for a in range(3):
        for b in range(3):
            tap = 3 * a + b
            patch_ref[:, tap * chans : (tap + 1) * chans] = pad_ref[
                b, a * width : a * width + cells, :
            ]


def exponent(top):
    power = jnp.ones_like(top)
    count = jnp.zeros_like(top)
    for step in STEPS:
        fits = top * (2.0**step) < 32768.0
        factor = jnp.where(fits, 2.0**step, 1.0)
        top = top * factor
        power = power * factor
        count = count + jnp.where(fits, float(step), 0.0)
    return power, count


def inverse(count):
    power = jnp.ones_like(count)
    for step in STEPS:
        has = count >= step
        power = power * jnp.where(has, 2.0**-step, 1.0)
        count = count - jnp.where(has, float(step), 0.0)
    return power


def split_by_core(share, core, cot_ref, out_ref):
    rows, channels = cot_ref.shape
    half = channels // 2
    source = lax.broadcasted_iota(jnp.int32, (256, 128), 0)
    target = lax.broadcasted_iota(jnp.int32, (256, 128), 1)
    place = (target // share) * (2 * share) + lax.rem(target, share)
    top = jnp.max(jnp.abs(cot_ref[...].astype(F32)), axis=0, keepdims=True)
    top = jnp.max(top, axis=1, keepdims=True)
    power, count = exponent(jnp.broadcast_to(top, (8, half)))
    for slot, owner in ((0, 1 - core), (1, core)):
        pick = jnp.where(source == place + owner * share, 1.0, 0.0).astype(BF16)
        for k in range(half // 128):
            value = jnp.dot(
                cot_ref[:, 256 * k : 256 * (k + 1)], pick, preferred_element_type=F32
            )
            out_ref[slot * rows : (slot + 1) * rows, 128 * k : 128 * (k + 1)] = (
                value * power[:1, :128]
            )
    out_ref[2 * rows :, :] = count


def forward_kernel(width, share, core_ref, x_ref, cot_ref, kernel_ref, *refs):
    out_ref, both_ref, patch_ref, pad_ref, held_ref, sem = refs
    block = out_ref.shape[1]

    @pl.when(pl.program_id(0) == 0)
    def _():
        copy = pltpu.make_async_copy(kernel_ref, held_ref, sem)
        copy.start()
        build_patches(width, x_ref, pad_ref, patch_ref)
        split_by_core(share, core_ref[0], cot_ref, both_ref)
        copy.wait()

    columns = pl.ds(pl.multiple_of(pl.program_id(0) * block, block), block)
    out_ref[...] = jnp.dot(patch_ref[...], held_ref[:, columns], preferred_element_type=F32)


def forward_partial(width, share, core, x, cot, weights):
    cells, chans = x.shape
    taps, channels = weights.shape
    rows = 2 * cot.shape[0] + 8
    block = channels // 2
    x = pltpu.with_memory_space_constraint(x, pltpu.HBM)
    cot = pltpu.with_memory_space_constraint(cot, pltpu.HBM)
    weights = pltpu.with_memory_space_constraint(weights, pltpu.HBM)
    return pl.pallas_call(
        functools.partial(forward_kernel, width, share),
        out_shape=(
            pltpu.HBM((cells, channels), F32),
            jax.ShapeDtypeStruct((rows, channels // 2), F32),
            jax.ShapeDtypeStruct((cells, taps), BF16),
        ),
        grid=(2,),
        in_specs=[
            pl.BlockSpec(memory_space=pltpu.SMEM),
            pl.BlockSpec((cells, chans), lambda i: (0, 0)),
            pl.BlockSpec(cot.shape, lambda i: (0, 0)),
            pl.BlockSpec(memory_space=pl.ANY),
        ],
        out_specs=(
            pl.BlockSpec((cells, block), lambda i: (0, i)),
            pl.BlockSpec((rows, channels // 2), lambda i: (0, 0)),
            pl.BlockSpec((cells, taps), lambda i: (0, 0)),
        ),
        scratch_shapes=[
            pltpu.VMEM((3, cells + 2 * width, chans), BF16),
            pltpu.VMEM((taps, channels), BF16),
            pltpu.SemaphoreType.DMA,
        ],
        compiler_params=pltpu.CompilerParams(vmem_limit_bytes=26 << 20),
        name="forward",
    )(core, x, cot, weights)


def multiply_turned(scale, cot, patch_ref, grad_ref, turned_ref):
    turned = cot.T
    turned_ref[...] = turned
    grad = scale * jnp.dot(turned, patch_ref[...], preferred_element_type=F32)
    chips, rows, chans = grad_ref.shape
    share = rows // 9
    for chip in range(chips):
        for tap in range(9):
            grad_ref[chip, tap * share : (tap + 1) * share, :] = grad[
                chip * share : (chip + 1) * share, tap * chans : (tap + 1) * chans
            ]


def first_kernel(scale, patch_ref, all_ref, grad_ref, turned_ref, cot_ref, mine_ref):
    groups = all_ref.shape[0]
    rows = (all_ref.shape[1] - 8) // 2
    for group in range(groups):
        power = inverse(all_ref[group, 2 * rows :, :].astype(F32))[:1]
        for slot, ref in ((0, cot_ref), (1, mine_ref)):
            value = all_ref[group, slot * rows : (slot + 1) * rows, :].astype(F32) * power
            ref[group * rows : (group + 1) * rows, :] = value.astype(BF16)
    start = cot_ref[:, : turned_ref.shape[0]]
    multiply_turned(scale, start, patch_ref, grad_ref, turned_ref)


def weight_first(scale, share, patches, gathered):
    cells = patches.shape[0]
    chans = patches.shape[1] // 9
    half = gathered.shape[2]
    vmem = pl.BlockSpec(memory_space=pltpu.VMEM)
    return pl.pallas_call(
        functools.partial(first_kernel, scale),
        out_shape=(
            jax.ShapeDtypeStruct((half // 2 // share, 9 * share, chans), F32),
            pltpu.HBM((half // 2, cells), BF16),
            jax.ShapeDtypeStruct((cells, half), BF16),
            jax.ShapeDtypeStruct((cells, half), BF16),
        ),
        in_specs=[vmem, vmem],
        out_specs=(vmem,) * 4,
        compiler_params=pltpu.CompilerParams(vmem_limit_bytes=24 << 20),
        name="weight_first",
    )(patches, gathered)


def second_kernel(scale, cot_ref, patch_ref, grad_ref, turned_ref):
    multiply_turned(scale, cot_ref[...], patch_ref, grad_ref, turned_ref)


def weight_second(scale, share, cot, patches, parts, part):
    cells = cot.shape[0]
    half = cot.shape[1] // parts
    chans = patches.shape[1] // 9
    vmem = pl.BlockSpec(memory_space=pltpu.VMEM)
    return pl.pallas_call(
        functools.partial(second_kernel, scale),
        out_shape=(
            jax.ShapeDtypeStruct((half // share, 9 * share, chans), F32),
            pltpu.HBM((half, cells), BF16),
        ),
        grid=(1,),
        in_specs=[pl.BlockSpec((cells, half), lambda i: (0, part)), vmem],
        out_specs=(vmem, vmem),
        compiler_params=pltpu.CompilerParams(vmem_limit_bytes=24 << 20),
        name="weight_second",
    )(cot, patches)


def input_kernel(width, share, core_ref, *refs):
    early_ref, late_ref, mine_ref, kernel_ref, out_ref, cot_ref = refs
    cells, chans = out_ref.shape
    core = core_ref[0]
    middle = early_ref.shape[0] // share
    for ref, owner, first in (
        (early_ref, 1 - core, 0),
        (late_ref, 1 - core, middle),
        (mine_ref, core, 0),
    ):
        for chip in range(ref.shape[0] // share):
            start = pl.multiple_of((2 * (first + chip) + owner) * share, share)
            cot_ref[pl.ds(start, share), :] = ref[chip * share : (chip + 1) * share, :]
    spread = jnp.dot(kernel_ref[...], cot_ref[...], preferred_element_type=F32)
    cell = lax.broadcasted_iota(jnp.int32, (chans, cells), 1)
    column = lax.rem(cell, width)
    total = None
    for b in range(3):
        part = None
        for a in range(3):
            tap = 3 * a + b
            term = spread[tap * chans : (tap + 1) * chans, :]
            if a == 0:
                term = jnp.where(cell < cells - width, pltpu.roll(term, cells - width, 1), 0.0)
            if a == 2:
                term = jnp.where(cell >= width, pltpu.roll(term, width, 1), 0.0)
            part = term if part is None else part + term
        if b == 0:
            part = jnp.where(column < width - 1, pltpu.roll(part, cells - 1, 1), 0.0)
        if b == 2:
            part = jnp.where(column > 0, pltpu.roll(part, 1, 1), 0.0)
        total = part if total is None else total + part
    out_ref[...] = total.T.astype(BF16)


def input_gradient(width, share, core, early, late, mine, weights):
    cells = mine.shape[1]
    chans = weights.shape[0] // 9
    vmem = pl.BlockSpec(memory_space=pltpu.VMEM)
    return pl.pallas_call(
        functools.partial(input_kernel, width, share),
        out_shape=jax.ShapeDtypeStruct((cells, chans), BF16),
        in_specs=[pl.BlockSpec(memory_space=pltpu.SMEM)] + [vmem] * 4,
        out_specs=vmem,
        scratch_shapes=[pltpu.VMEM((weights.shape[1], cells), BF16)],
        compiler_params=pltpu.CompilerParams(vmem_limit_bytes=24 << 20),
        name="input_grad",
    )(core, early, late, mine, weights)


def shrink(value):
    rows = value.shape[1]
    power, count = exponent(jnp.max(jnp.abs(value), axis=(1, 2), keepdims=True))
    wide = jnp.pad(value, ((0, 0), (0, 8), (0, 0)))
    row = lax.broadcasted_iota(jnp.int32, wide.shape, 1)
    return jnp.where(row < rows, wide * power, count).astype(F16)


def grow(packed):
    power = inverse(packed[:, -8:-7, :].astype(F32))
    return packed[:, :-8].astype(F32) * power


def on_device(inputs, kernel, cotangent):
    height, width, local_in = inputs.shape[1:]
    channels = kernel.shape[3]
    groups = lax.axis_size("filter")
    chips = lax.axis_size("chip")
    samples = chips * lax.axis_size("core")
    share = channels // samples
    cells = height * width
    x = inputs.reshape(cells, local_in)
    weights = kernel.reshape(9 * local_in, channels)
    rows = cells // groups
    cot = cotangent.reshape(rows, channels)
    core = lax.axis_index("core").astype(jnp.int32).reshape(1)
    scale = 1.0 / float(samples * cells) ** 0.5

    partial, both, patches = forward_partial(width, share, core, x, cot, weights)
    summed = lax.psum_scatter(partial, "filter", scatter_dimension=0, tiled=True)
    outputs = summed.astype(BF16).reshape(cotangent.shape)
    gathered = lax.all_gather(both.astype(F16), "filter", axis=0).astype(BF16)
    swap = [(0, 1), (1, 0)]
    early, early_turned, theirs, mine = weight_first(scale, share, patches, gathered)
    early = lax.ppermute(early, "core", swap)
    late, late_turned = weight_second(scale, share, theirs, patches, 2, 1)
    late = lax.ppermute(late, "core", swap)
    mine_grad, mine_turned = weight_second(scale, share, mine, patches, 1, 0)
    packed = shrink(mine_grad + jnp.concatenate([early, late], axis=0))
    input_grad = input_gradient(
        width, share, core, early_turned, late_turned, mine_turned, weights
    )
    input_grad = input_grad.reshape(inputs.shape)

    packed = lax.all_to_all(packed, "chip", 0, 0, tiled=True)
    packed, outputs = lax.optimization_barrier((packed, outputs))
    kernel_grad = jnp.sum(grow(packed), axis=0).reshape(9, share, local_in)
    kernel_grad = kernel_grad.transpose(1, 0, 2)
    return (outputs, input_grad, kernel_grad.reshape(share, 3, 3, local_in))


def solution(mesh):
    samples, groups = mesh.devices.shape
    split = Mesh(
        mesh.devices.reshape(samples // 2, 2, groups), ("chip", "core", "filter")
    )
    dp = ("chip", "core")
    return jax.shard_map(
        on_device,
        mesh=split,
        in_specs=(
            P(dp, None, None, "filter"),
            P(None, None, "filter", None),
            P(dp, "filter", None, None),
        ),
        out_specs=(
            P(dp, "filter", None, None),
            P(dp, None, None, "filter"),
            P(dp, None, None, "filter"),
        ),
        check_vma=False,
    )
```

```python
import functools

import jax
import jax.numpy as jnp
from jax import lax
from jax.experimental import pallas as pl
from jax.experimental.pallas import tpu as pltpu
from jax.sharding import Mesh, PartitionSpec as P

F32 = jnp.float32
BF16 = jnp.bfloat16
F16 = jnp.float16
STEPS = (64, 32, 16, 8, 4, 2, 1)


def build_patches(width, x_ref, pad_ref, patch_ref):
    cells, chans = x_ref.shape
    value = x_ref[...].astype(F32)
    column = lax.rem(lax.broadcasted_iota(jnp.int32, value.shape, 0), width)
    left = jnp.where(column == 0, 0.0, pltpu.roll(value, 1, 0))
    right = jnp.where(column == width - 1, 0.0, pltpu.roll(value, cells - 1, 0))
    for b, shifted in enumerate((left, value, right)):
        pad_ref[b, :width, :] = jnp.zeros((width, chans), BF16)
        pad_ref[b, width : width + cells, :] = shifted.astype(BF16)
        pad_ref[b, width + cells :, :] = jnp.zeros((width, chans), BF16)
    for a in range(3):
        for b in range(3):
            tap = 3 * a + b
            patch_ref[:, tap * chans : (tap + 1) * chans] = pad_ref[
                b, a * width : a * width + cells, :
            ]


def exponent(top):
    power = jnp.ones_like(top)
    count = jnp.zeros_like(top)
    for step in STEPS:
        fits = top * (2.0**step) < 32768.0
        factor = jnp.where(fits, 2.0**step, 1.0)
        top = top * factor
        power = power * factor
        count = count + jnp.where(fits, float(step), 0.0)
    return power, count


def inverse(count):
    power = jnp.ones_like(count)
    for step in STEPS:
        has = count >= step
        power = power * jnp.where(has, 2.0**-step, 1.0)
        count = count - jnp.where(has, float(step), 0.0)
    return power


def split_by_core(share, core, cot_ref, out_ref):
    rows, channels = cot_ref.shape
    half = channels // 2
    source = lax.broadcasted_iota(jnp.int32, (256, 128), 0)
    target = lax.broadcasted_iota(jnp.int32, (256, 128), 1)
    place = (target // share) * (2 * share) + lax.rem(target, share)
    top = jnp.max(jnp.abs(cot_ref[...].astype(F32)), axis=0, keepdims=True)
    top = jnp.max(top, axis=1, keepdims=True)
    power, count = exponent(jnp.broadcast_to(top, (8, half)))
    for slot, owner in ((0, 1 - core), (1, core)):
        pick = jnp.where(source == place + owner * share, 1.0, 0.0).astype(BF16)
        for k in range(half // 128):
            value = jnp.dot(
                cot_ref[:, 256 * k : 256 * (k + 1)], pick, preferred_element_type=F32
            )
            out_ref[slot * rows : (slot + 1) * rows, 128 * k : 128 * (k + 1)] = (
                value * power[:1, :128]
            )
    out_ref[2 * rows :, :] = count


def forward_kernel(width, share, core_ref, x_ref, cot_ref, kernel_ref, *refs):
    out_ref, both_ref, patch_ref, pad_ref, held_ref, sem = refs
    block = out_ref.shape[1]

    @pl.when(pl.program_id(0) == 0)
    def _():
        copy = pltpu.make_async_copy(kernel_ref, held_ref, sem)
        copy.start()
        build_patches(width, x_ref, pad_ref, patch_ref)
        split_by_core(share, core_ref[0], cot_ref, both_ref)
        copy.wait()

    columns = pl.ds(pl.multiple_of(pl.program_id(0) * block, block), block)
    out_ref[...] = jnp.dot(patch_ref[...], held_ref[:, columns], preferred_element_type=F32)


def forward_partial(width, share, core, x, cot, weights):
    cells, chans = x.shape
    taps, channels = weights.shape
    rows = 2 * cot.shape[0] + 8
    block = channels // 4
    x = pltpu.with_memory_space_constraint(x, pltpu.HBM)
    cot = pltpu.with_memory_space_constraint(cot, pltpu.HBM)
    weights = pltpu.with_memory_space_constraint(weights, pltpu.HBM)
    return pl.pallas_call(
        functools.partial(forward_kernel, width, share),
        out_shape=(
            pltpu.HBM((cells, channels), F32),
            jax.ShapeDtypeStruct((rows, channels // 2), F32),
            jax.ShapeDtypeStruct((cells, taps), BF16),
        ),
        grid=(4,),
        in_specs=[
            pl.BlockSpec(memory_space=pltpu.SMEM),
            pl.BlockSpec((cells, chans), lambda i: (0, 0)),
            pl.BlockSpec(cot.shape, lambda i: (0, 0)),
            pl.BlockSpec(memory_space=pl.ANY),
        ],
        out_specs=(
            pl.BlockSpec((cells, block), lambda i: (0, i)),
            pl.BlockSpec((rows, channels // 2), lambda i: (0, 0)),
            pl.BlockSpec((cells, taps), lambda i: (0, 0)),
        ),
        scratch_shapes=[
            pltpu.VMEM((3, cells + 2 * width, chans), BF16),
            pltpu.VMEM((taps, channels), BF16),
            pltpu.SemaphoreType.DMA,
        ],
        compiler_params=pltpu.CompilerParams(vmem_limit_bytes=26 << 20),
        name="forward",
    )(core, x, cot, weights)


def multiply_turned(scale, cot, patch_ref, grad_ref, turned_ref):
    turned = cot.T
    turned_ref[...] = turned
    grad = scale * jnp.dot(turned, patch_ref[...], preferred_element_type=F32)
    chips, rows, chans = grad_ref.shape
    share = rows // 9
    for chip in range(chips):
        for tap in range(9):
            grad_ref[chip, tap * share : (tap + 1) * share, :] = grad[
                chip * share : (chip + 1) * share, tap * chans : (tap + 1) * chans
            ]


def first_kernel(scale, patch_ref, all_ref, grad_ref, turned_ref, cot_ref, mine_ref):
    groups = all_ref.shape[0]
    rows = (all_ref.shape[1] - 8) // 2
    for group in range(groups):
        power = inverse(all_ref[group, 2 * rows :, :].astype(F32))[:1]
        for slot, ref in ((0, cot_ref), (1, mine_ref)):
            value = all_ref[group, slot * rows : (slot + 1) * rows, :].astype(F32) * power
            ref[group * rows : (group + 1) * rows, :] = value.astype(BF16)
    start = cot_ref[:, : turned_ref.shape[0]]
    multiply_turned(scale, start, patch_ref, grad_ref, turned_ref)


def weight_first(scale, share, patches, gathered):
    cells = patches.shape[0]
    chans = patches.shape[1] // 9
    half = gathered.shape[2]
    vmem = pl.BlockSpec(memory_space=pltpu.VMEM)
    return pl.pallas_call(
        functools.partial(first_kernel, scale),
        out_shape=(
            jax.ShapeDtypeStruct((half // 2 // share, 9 * share, chans), F32),
            pltpu.HBM((half // 2, cells), BF16),
            jax.ShapeDtypeStruct((cells, half), BF16),
            jax.ShapeDtypeStruct((cells, half), BF16),
        ),
        in_specs=[vmem, vmem],
        out_specs=(vmem,) * 4,
        compiler_params=pltpu.CompilerParams(vmem_limit_bytes=24 << 20),
        name="weight_first",
    )(patches, gathered)


def second_kernel(scale, cot_ref, patch_ref, grad_ref, turned_ref):
    multiply_turned(scale, cot_ref[...], patch_ref, grad_ref, turned_ref)


def weight_second(scale, share, cot, patches, parts, part):
    cells = cot.shape[0]
    half = cot.shape[1] // parts
    chans = patches.shape[1] // 9
    vmem = pl.BlockSpec(memory_space=pltpu.VMEM)
    return pl.pallas_call(
        functools.partial(second_kernel, scale),
        out_shape=(
            jax.ShapeDtypeStruct((half // share, 9 * share, chans), F32),
            pltpu.HBM((half, cells), BF16),
        ),
        grid=(1,),
        in_specs=[pl.BlockSpec((cells, half), lambda i: (0, part)), vmem],
        out_specs=(vmem, vmem),
        compiler_params=pltpu.CompilerParams(vmem_limit_bytes=24 << 20),
        name="weight_second",
    )(cot, patches)


def input_kernel(width, share, core_ref, *refs):
    early_ref, late_ref, mine_ref, kernel_ref, out_ref, cot_ref = refs
    cells, chans = out_ref.shape
    core = core_ref[0]
    middle = early_ref.shape[0] // share
    for ref, owner, first in (
        (early_ref, 1 - core, 0),
        (late_ref, 1 - core, middle),
        (mine_ref, core, 0),
    ):
        for chip in range(ref.shape[0] // share):
            start = pl.multiple_of((2 * (first + chip) + owner) * share, share)
            cot_ref[pl.ds(start, share), :] = ref[chip * share : (chip + 1) * share, :]
    spread = jnp.dot(kernel_ref[...], cot_ref[...], preferred_element_type=F32)
    cell = lax.broadcasted_iota(jnp.int32, (chans, cells), 1)
    column = lax.rem(cell, width)
    total = None
    for b in range(3):
        part = None
        for a in range(3):
            tap = 3 * a + b
            term = spread[tap * chans : (tap + 1) * chans, :]
            if a == 0:
                term = jnp.where(cell < cells - width, pltpu.roll(term, cells - width, 1), 0.0)
            if a == 2:
                term = jnp.where(cell >= width, pltpu.roll(term, width, 1), 0.0)
            part = term if part is None else part + term
        if b == 0:
            part = jnp.where(column < width - 1, pltpu.roll(part, cells - 1, 1), 0.0)
        if b == 2:
            part = jnp.where(column > 0, pltpu.roll(part, 1, 1), 0.0)
        total = part if total is None else total + part
    out_ref[...] = total.T.astype(BF16)


def input_gradient(width, share, core, early, late, mine, weights):
    cells = mine.shape[1]
    chans = weights.shape[0] // 9
    vmem = pl.BlockSpec(memory_space=pltpu.VMEM)
    return pl.pallas_call(
        functools.partial(input_kernel, width, share),
        out_shape=jax.ShapeDtypeStruct((cells, chans), BF16),
        in_specs=[pl.BlockSpec(memory_space=pltpu.SMEM)] + [vmem] * 4,
        out_specs=vmem,
        scratch_shapes=[pltpu.VMEM((weights.shape[1], cells), BF16)],
        compiler_params=pltpu.CompilerParams(vmem_limit_bytes=24 << 20),
        name="input_grad",
    )(core, early, late, mine, weights)


def shrink(value):
    rows = value.shape[1]
    power, count = exponent(jnp.max(jnp.abs(value), axis=(1, 2), keepdims=True))
    wide = jnp.pad(value, ((0, 0), (0, 8), (0, 0)))
    row = lax.broadcasted_iota(jnp.int32, wide.shape, 1)
    return jnp.where(row < rows, wide * power, count).astype(F16)


def grow(packed):
    power = inverse(packed[:, -8:-7, :].astype(F32))
    return packed[:, :-8].astype(F32) * power


def on_device(inputs, kernel, cotangent):
    height, width, local_in = inputs.shape[1:]
    channels = kernel.shape[3]
    groups = lax.axis_size("filter")
    chips = lax.axis_size("chip")
    samples = chips * lax.axis_size("core")
    share = channels // samples
    cells = height * width
    x = inputs.reshape(cells, local_in)
    weights = kernel.reshape(9 * local_in, channels)
    rows = cells // groups
    cot = cotangent.reshape(rows, channels)
    core = lax.axis_index("core").astype(jnp.int32).reshape(1)
    scale = 1.0 / float(samples * cells) ** 0.5

    partial, both, patches = forward_partial(width, share, core, x, cot, weights)
    summed = lax.psum_scatter(partial, "filter", scatter_dimension=0, tiled=True)
    outputs = summed.astype(BF16).reshape(cotangent.shape)
    gathered = lax.all_gather(both.astype(F16), "filter", axis=0).astype(BF16)
    swap = [(0, 1), (1, 0)]
    early, early_turned, theirs, mine = weight_first(scale, share, patches, gathered)
    early = lax.ppermute(early, "core", swap)
    late, late_turned = weight_second(scale, share, theirs, patches, 2, 1)
    late = lax.ppermute(late, "core", swap)
    mine_grad, mine_turned = weight_second(scale, share, mine, patches, 1, 0)
    packed = shrink(mine_grad + jnp.concatenate([early, late], axis=0))
    input_grad = input_gradient(
        width, share, core, early_turned, late_turned, mine_turned, weights
    )
    input_grad = input_grad.reshape(inputs.shape)

    packed = lax.all_to_all(packed, "chip", 0, 0, tiled=True)
    packed, outputs = lax.optimization_barrier((packed, outputs))
    kernel_grad = jnp.sum(grow(packed), axis=0).reshape(9, share, local_in)
    kernel_grad = kernel_grad.transpose(1, 0, 2)
    return (outputs, input_grad, kernel_grad.reshape(share, 3, 3, local_in))


def solution(mesh):
    samples, groups = mesh.devices.shape
    split = Mesh(
        mesh.devices.reshape(samples // 2, 2, groups), ("chip", "core", "filter")
    )
    dp = ("chip", "core")
    return jax.shard_map(
        on_device,
        mesh=split,
        in_specs=(
            P(dp, None, None, "filter"),
            P(None, None, "filter", None),
            P(dp, "filter", None, None),
        ),
        out_specs=(
            P(dp, "filter", None, None),
            P(dp, None, None, "filter"),
            P(dp, None, None, "filter"),
        ),
        check_vma=False,
    )
```
